1024 devices in a mesh: dp: 64 (over z, y_lo), mp: 16 (over x, y_hi, core).
Axes of the slice: x: 4, y: 4 (y_hi: 2, y_lo: 2; y = y_hi * 2 + y_lo), z: 32, core: 2. Of those that a mesh axis runs over, the one named last changes fastest.
Arguments:
- layer_input: bfloat16 [64, 16, 8, 32, 256], P('dp', 'mp'), may hold values from -6 to 6
- hidden_pre: bfloat16 [64, 16, 8, 32, 256], P('dp', 'mp'), may hold values from -6 to 6
- out_grad: bfloat16 [64, 16, 8, 32, 256], P('dp', 'mp'), may hold values from -0.03125 to 0.03125
- weight_second: bfloat16 [256, 6912], replicated, may hold values from -0.078125 to 0.078125
Outputs:
- grad_second: float32 [256, 6912], P('mp')
- grad_first: float32 [256, 6912], P('mp')
The draws below stay inside these ranges and needn't reach their ends.
All inputs are finite; a program needn't handle non-finite values.
Results may differ from the reference program's by a relative error of at most 0.0029.
Values may be sent and summed in bfloat16 or wider, within the bound.
No kernel may reach another device: no remote copies, remote signals or barrier semaphores. Data moves between devices by JAX's collectives and lax.ppermute only.
A program may use at most 32 MiB of HBM per device.

```python
import jax
import jax.numpy as jnp
from jax import lax

C = 256
KVOL = 27
SY = 8
SZ = 32
SX = 16
BATCH = 64


def levels(rng, shape, pieces, least, top_value):
    gain, own = 1.0, jax.random.fold_in(rng, 6)
    for dim, blocks in pieces:
        draws = jnp.exp(jax.random.uniform(jax.random.fold_in(own, dim), (blocks,), jnp.float32, least / len(pieces), top_value / len(pieces)))
        gain = gain * jnp.repeat(draws, shape[dim] // blocks).reshape([-1 if axis == dim else 1 for axis in range(len(shape))])
    return gain


def centred(key, extent, deviation, reach, pieces=(), kind=jnp.bfloat16):
    level = levels(key, extent, pieces, -0.22, 0.18) if pieces else 1.0
    entries = jax.random.normal(key, extent, jnp.float32) * deviation * level
    return jnp.minimum(jnp.maximum(entries, -reach), reach).astype(kind)


def setup_inputs(seed: int = 0) -> dict:
    keys = jax.random.split(jax.random.key(seed), 5)
    return {
        "layer_input": centred(keys[0], (BATCH, SX, SY, SZ, C), 1.0, 6.0, ((0, 64), (1, 16))),
        "hidden_pre": centred(keys[1], (BATCH, SX, SY, SZ, C), 1.0, 6.0, ((0, 64), (1, 16))),
        "out_grad": centred(keys[2], (BATCH, SX, SY, SZ, C), 0.005, 0.03125, ((0, 64), (1, 16))),
        "weight_second": centred(keys[3], (C, KVOL * C), (KVOL * C) ** -0.5, 0.078125),
    }


def forward_taps(volume):
    padded = jnp.pad(volume, ((1, 1), (1, 1), (1, 1), (0, 0)))
    depth, height, width, chans = volume.shape
    columns = []
    for shift_x in range(3):
        for shift_y in range(3):
            for shift_z in range(3):
                columns.append(padded[shift_x:shift_x + depth, shift_y:shift_y + height, shift_z:shift_z + width])
    return jnp.stack(columns, 3).reshape(depth * height * width, 27, chans)

def backward_taps(volume):
    padded = jnp.pad(volume, ((1, 1), (1, 1), (1, 1), (0, 0)))
    depth, height, width, chans = volume.shape
    columns = []
    for shift_x in range(3):
        for shift_y in range(3):
            for shift_z in range(3):
                columns.append(padded[2 - shift_x:2 - shift_x + depth, 2 - shift_y:2 - shift_y + height, 2 - shift_z:2 - shift_z + width])
    return jnp.stack(columns, 3).reshape(depth * height * width, 27, chans)

def kernel_grad(inputs, grads):
    chans = inputs.shape[-1]
    taps = forward_taps(inputs.astype(jnp.float32))
    flat_grad = grads.astype(jnp.float32).reshape(-1, chans)
    return jnp.einsum('vc,vki->cki', flat_grad, taps).reshape(chans, 27 * chans)

def reference(layer_input, hidden_pre, out_grad, weight_second):
    chans = weight_second.shape[0]
    kernel = weight_second.astype(jnp.float32).reshape(chans, 27, chans)

    def per_sample(carry, sample):
        first_in, pre, grad = sample
        second_input = jnp.maximum(pre, 0)
        grad_two = carry[0] + kernel_grad(second_input, grad)
        taps = backward_taps(grad.astype(jnp.float32))
        input_grad = jnp.einsum('vkc,cki->vi', taps, kernel).reshape(pre.shape)
        hidden_grad = jnp.where(pre > 0, input_grad, 0.0).astype(jnp.bfloat16)
        grad_one = carry[1] + kernel_grad(first_in, hidden_grad)
        return ((grad_two, grad_one), None)
    start = (jnp.zeros((chans, 27 * chans), jnp.float32), jnp.zeros((chans, 27 * chans), jnp.float32))
    totals, unused = lax.scan(per_sample, start, (layer_input, hidden_pre, out_grad))
    return (totals[0], totals[1])
```

```python
import jax
import jax.numpy as jnp
from jax import lax
from jax.experimental import pallas as pl
from jax.experimental.pallas import tpu as pltpu
from jax.sharding import Mesh, PartitionSpec as P

F32 = jnp.float32
BF16 = jnp.bfloat16
PLANES = 16
ROWS = 8
COLS = 32
VOX = ROWS * COLS
CHANS = 256
BLK = 64
LINES = 216
PADDED = 224
PIECE = 56

VMEM = pl.BlockSpec(memory_space=pltpu.VMEM)
PARAMS = pltpu.CompilerParams(vmem_limit_bytes=48 * 1024 * 1024)


def shifted(value, step, axis):
    size = value.shape[axis]
    return pltpu.roll(value, (-step) % size, axis)


def spread_kernel(grad_ref, pre_ref, first_ref, out_ref):
    grad = grad_ref[...].reshape(VOX, CHANS).T
    second = jnp.maximum(pre_ref[...].reshape(VOX, CHANS), 0).T
    first = first_ref[...].reshape(VOX, CHANS).T
    for x in range(4):
        for q in range(4):
            dest = x * 4 + q
            out_ref[dest, 0:BLK] = grad[BLK * x : BLK * (x + 1)]
            out_ref[dest, BLK : 2 * BLK] = second[BLK * q : BLK * (q + 1)]
            out_ref[dest, 2 * BLK : 3 * BLK] = first[BLK * q : BLK * (q + 1)]


def spread(grad, pre, first):
    return pl.pallas_call(
        spread_kernel,
        out_shape=jax.ShapeDtypeStruct((PLANES, 3 * BLK, VOX), BF16),
        in_specs=[VMEM] * 3,
        out_specs=VMEM,
        compiler_params=PARAMS,
        name="spread",
    )(grad, pre, first)


def data_grad_kernel(low_ref, own_ref, high_ref, pre_ref, weight_ref, out_ref, held, moved, sems):
    def copy(part):
        columns = pl.ds(part * 3 * CHANS, 3 * CHANS)
        return pltpu.make_async_copy(
            weight_ref.at[:, columns], held.at[part], sems.at[part]
        )

    for part in range(9):
        copy(part).start()
    col = lax.broadcasted_iota(jnp.int32, (VOX, CHANS), 0) % COLS
    blank = jnp.zeros((COLS, CHANS), BF16)
    for a, source in enumerate((high_ref, own_ref, low_ref)):
        plane = source[...].reshape(VOX, CHANS)
        wide = plane.astype(F32)
        views = (
            jnp.where(col < COLS - 1, shifted(wide, 1, 0), 0.0).astype(BF16),
            plane,
            jnp.where(col > 0, shifted(wide, -1, 0), 0.0).astype(BF16),
        )
        for c in range(3):
            moved[a, c, 0:COLS] = blank
            moved[a, c, COLS : COLS + VOX] = views[c]
            moved[a, c, COLS + VOX : 2 * COLS + VOX] = blank
    total = jnp.zeros((VOX, CHANS), F32)
    for a in range(3):
        for b in range(3):
            part = a * 3 + b
            copy(part).wait()
            for c in range(3):
                total = total + jnp.dot(
                    moved[a, c, (2 - b) * COLS : (2 - b) * COLS + VOX],
                    held[part, :, c * CHANS : (c + 1) * CHANS],
                    preferred_element_type=F32,
                )
    pre = pre_ref[...].reshape(VOX, CHANS)
    hidden = jnp.where(pre > 0, total, 0.0).astype(BF16).T
    for x in range(4):
        for q in range(4):
            out_ref[x * 4 + q] = hidden[BLK * x : BLK * (x + 1)]


def data_grad(low, own, high, pre, weight):
    return pl.pallas_call(
        data_grad_kernel,
        out_shape=jax.ShapeDtypeStruct((PLANES, BLK, VOX), BF16),
        in_specs=[VMEM] * 4 + [pl.BlockSpec(memory_space=pl.ANY)],
        out_specs=VMEM,
        scratch_shapes=[
            pltpu.VMEM((9, CHANS, 3 * CHANS), BF16),
            pltpu.VMEM((3, 3, VOX + 2 * COLS, CHANS), BF16),
            pltpu.SemaphoreType.DMA((9,)),
        ],
        compiler_params=PARAMS,
        cost_estimate=pl.CostEstimate(
            flops=2 * VOX * 27 * CHANS * CHANS, bytes_accessed=4 * 1024 * 1024, transcendentals=0
        ),
        name="data_grad",
    )(low, own, high, pre, weight)


def weight_grad_kernel(grad_ref, act_ref, out_ref, grads, acts):
    lane = lax.broadcasted_iota(jnp.int32, (BLK, VOX), 1)
    row, col = lane // COLS, lane % COLS
    for plane in range(PLANES):
        here = slice(plane * VOX, (plane + 1) * VOX)
        act = act_ref[plane]
        wide = act.astype(F32)
        acts[0:BLK, here] = jnp.where(col > 0, shifted(wide, -1, 1), 0.0).astype(BF16)
        acts[BLK : 2 * BLK, here] = act
        acts[2 * BLK : 3 * BLK, here] = jnp.where(
            col < COLS - 1, shifted(wide, 1, 1), 0.0
        ).astype(BF16)
        grad = grad_ref[plane]
        wide = grad.astype(F32)
        views = (
            jnp.where(row < ROWS - 1, shifted(wide, COLS, 1), 0.0).astype(BF16),
            grad,
            jnp.where(row > 0, shifted(wide, -COLS, 1), 0.0).astype(BF16),
        )
        for a in range(3):
            there = plane + a - 1
            if 0 <= there < PLANES:
                for b in range(3):
                    top = (a * 3 + b) * BLK
                    grads[top : top + BLK, there * VOX : (there + 1) * VOX] = views[b]
    blank = jnp.zeros((3 * BLK, VOX), BF16)
    grads[0 : 3 * BLK, (PLANES - 1) * VOX : PLANES * VOX] = blank
    grads[6 * BLK : 9 * BLK, 0:VOX] = blank
    total = lax.dot_general(
        grads[...], acts[...], (((1,), (1,)), ((), ())), preferred_element_type=F32
    )
    for part in range(4):
        pieces = [total[k * BLK + part * 16 : k * BLK + part * 16 + 16] for k in range(9)]
        block = jnp.concatenate(pieces, axis=0)
        out_ref[part, 0:144] = block[:, 0:128].astype(out_ref.dtype)
        tail = block[:, 128:192]
        out_ref[part, 144:LINES] = jnp.concatenate([tail[0:72], tail[72:144]], axis=1).astype(
            out_ref.dtype
        )
        out_ref[part, LINES:PADDED] = jnp.zeros((PADDED - LINES, 128), out_ref.dtype)


def weight_grad(grads, grad_block, acts, act_block):
    return pl.pallas_call(
        weight_grad_kernel,
        out_shape=jax.ShapeDtypeStruct((4, PADDED, 128), F32),
        grid=(1,),
        in_specs=[
            pl.BlockSpec((PLANES, BLK, VOX), lambda i: (0, grad_block, 0)),
            pl.BlockSpec((PLANES, BLK, VOX), lambda i: (0, act_block, 0)),
        ],
        out_specs=pl.BlockSpec((4, PADDED, 128), lambda i: (0, 0, 0)),
        scratch_shapes=[
            pltpu.VMEM((9 * BLK, PLANES * VOX), BF16),
            pltpu.VMEM((3 * BLK, PLANES * VOX), BF16),
        ],
        compiler_params=PARAMS,
        cost_estimate=pl.CostEstimate(
            flops=2 * 27 * BLK * BLK * PLANES * VOX, bytes_accessed=2 * 1024 * 1024, transcendentals=0
        ),
        name="weight_grad",
    )(grads, acts)


def unpack_kernel(lines_ref, out_ref):
    for pair in range(2):
        tiles = [lines_ref[0, 2 * pair + side].astype(F32) for side in range(2)]
        heads = [tile[0:144] for tile in tiles]
        tails = [
            jnp.concatenate([tile[144:LINES, 0:BLK], tile[144:LINES, BLK:128]], axis=0)
            for tile in tiles
        ]
        planes = (
            jnp.concatenate([heads[0][:, 0:BLK], heads[1][:, 0:BLK]], axis=1),
            jnp.concatenate([heads[0][:, BLK:128], heads[1][:, BLK:128]], axis=1),
            jnp.concatenate([tails[0], tails[1]], axis=1),
        )
        for k in range(9):
            for c in range(3):
                start = (3 * k + c) * CHANS + pair * 128
                out_ref[:, start : start + 128] = planes[c][k * 16 : (k + 1) * 16]


def unpack(lines, which):
    return pl.pallas_call(
        unpack_kernel,
        out_shape=jax.ShapeDtypeStruct((16, 27 * CHANS), F32),
        grid=(1,),
        in_specs=[pl.BlockSpec((1, 4, PADDED, 128), lambda i: (which, 0, 0, 0))],
        out_specs=pl.BlockSpec((16, 27 * CHANS), lambda i: (0, 0)),
        compiler_params=PARAMS,
        name="unpack",
    )(lines)


def local(layer_input, hidden_pre, out_grad, weight_second):
    mp = ("x", "yh", "c")
    own = out_grad.reshape(ROWS, COLS, CHANS)
    pre = hidden_pre.reshape(ROWS, COLS, CHANS)
    first = layer_input.reshape(ROWS, COLS, CHANS)
    up = [(i, i + 1) for i in range(PLANES - 1)]
    low = lax.ppermute(own, mp, up)
    high = lax.ppermute(own, mp, [(b, a) for a, b in up])
    given = lax.all_to_all(spread(own, pre, first), mp, 0, 0, tiled=True)
    hidden = data_grad(low, own, high, pre, weight_second)
    hidden = lax.all_to_all(hidden, mp, 0, 0, tiled=True)
    second_part = weight_grad(given, 0, given, 1)
    first_part = weight_grad(hidden, 0, given, 2)
    parts = jnp.stack([second_part, first_part]).reshape(2, 2, 2, 2, 2, PIECE, 128)
    parts = parts.transpose(0, 3, 1, 4, 2, 5, 6).reshape(32, PIECE, 128)
    parts = lax.all_to_all(parts, ("zl", "yh", "yl", "c"), 0, 0, tiled=True)
    mine = parts.reshape(4, 2, 2, 2, PIECE, 128).sum((0, 2)).reshape(4, PIECE, 128)
    sums = lax.all_gather(mine, "zh", axis=0, tiled=False)
    mine = sums.sum(0).astype(BF16)
    lines = jnp.broadcast_to(mine[None], (8, 4, PIECE, 128))
    lines = lax.all_to_all(lines, ("zl", "yl"), 0, 0, tiled=True)
    lines = lines.reshape(2, 4, 4, PIECE, 128).transpose(0, 2, 1, 3, 4).reshape(2, 4, PADDED, 128)
    return unpack(lines, 0), unpack(lines, 1)


def solution(mesh):
    split = Mesh(mesh.devices.reshape(8, 4, 2, 4, 2, 2), ("zh", "zl", "yl", "x", "yh", "c"))
    dp, mp = ("zh", "zl", "yl"), ("x", "yh", "c")
    return jax.shard_map(
        local,
        mesh=split,
        in_specs=(P(dp, mp), P(dp, mp), P(dp, mp), P()),
        out_specs=(P(mp, None), P(mp, None)),
        check_vma=False,
    )
```

```python
import jax
import jax.numpy as jnp
from jax import lax
from jax.experimental import pallas as pl
from jax.experimental.pallas import tpu as pltpu
from jax.sharding import Mesh, PartitionSpec as P

F32 = jnp.float32
BF16 = jnp.bfloat16
F16 = jnp.float16
PLANES = 16
ROWS = 8
COLS = 32
VOX = ROWS * COLS
CHANS = 256
BLK = 64
LINES = 216
DATA = 54
PIECE = 56
TOP = 14.0

VMEM = pl.BlockSpec(memory_space=pltpu.VMEM)
PARAMS = pltpu.CompilerParams(vmem_limit_bytes=48 * 1024 * 1024)


def shifted(value, step, axis):
    size = value.shape[axis]
    return pltpu.roll(value, (-step) % size, axis)


def front_kernel(
    low_ref, own_ref, high_ref, pre_ref, first_ref, weight_ref, out_ref, held, moved, sems
):
    def copy(part):
        columns = pl.ds(part * 3 * CHANS, 3 * CHANS)
        return pltpu.make_async_copy(
            weight_ref.at[:, columns], held.at[part], sems.at[part]
        )

    for part in range(9):
        copy(part).start()
    col = lax.broadcasted_iota(jnp.int32, (VOX, CHANS), 0) % COLS
    blank = jnp.zeros((COLS, CHANS), BF16)
    for a, source in enumerate((high_ref, own_ref, low_ref)):
        plane = source[...].reshape(VOX, CHANS)
        wide = plane.astype(F32)
        views = (
            jnp.where(col < COLS - 1, shifted(wide, 1, 0), 0.0).astype(BF16),
            plane,
            jnp.where(col > 0, shifted(wide, -1, 0), 0.0).astype(BF16),
        )
        for c in range(3):
            moved[a, c, 0:COLS] = blank
            moved[a, c, COLS : COLS + VOX] = views[c]
            moved[a, c, COLS + VOX : 2 * COLS + VOX] = blank
    total = jnp.zeros((VOX, CHANS), F32)
    for a in range(3):
        for b in range(3):
            part = a * 3 + b
            copy(part).wait()
            for c in range(3):
                total = total + jnp.dot(
                    moved[a, c, (2 - b) * COLS : (2 - b) * COLS + VOX],
                    held[part, :, c * CHANS : (c + 1) * CHANS],
                    preferred_element_type=F32,
                )
    pre = pre_ref[...].reshape(VOX, CHANS)
    hidden = jnp.where(pre > 0, total, 0.0).astype(BF16).T
    grad = own_ref[...].reshape(VOX, CHANS).T
    second = jnp.maximum(pre, 0).T
    first = first_ref[...].reshape(VOX, CHANS).T
    for x in range(4):
        for q in range(4):
            dest = x * 4 + q
            out_ref[dest, 0:BLK] = grad[BLK * x : BLK * (x + 1)]
            out_ref[dest, BLK : 2 * BLK] = second[BLK * q : BLK * (q + 1)]
            out_ref[dest, 2 * BLK : 3 * BLK] = hidden[BLK * x : BLK * (x + 1)]
            out_ref[dest, 3 * BLK : 4 * BLK] = first[BLK * q : BLK * (q + 1)]


def front(low, own, high, pre, first, weight):
    return pl.pallas_call(
        front_kernel,
        out_shape=jax.ShapeDtypeStruct((PLANES, 4 * BLK, VOX), BF16),
        in_specs=[VMEM] * 5 + [pl.BlockSpec(memory_space=pltpu.HBM)],
        out_specs=VMEM,
        scratch_shapes=[
            pltpu.VMEM((9, CHANS, 3 * CHANS), BF16),
            pltpu.VMEM((3, 3, VOX + 2 * COLS, CHANS), BF16),
            pltpu.SemaphoreType.DMA((9,)),
        ],
        compiler_params=PARAMS,
        cost_estimate=pl.CostEstimate(
            flops=2 * VOX * 27 * CHANS * CHANS, bytes_accessed=4 * 1024 * 1024, transcendentals=0
        ),
        name="front",
    )(low, own, high, pre, first, weight)


def weight_grad_kernel(grad_ref, act_ref, out_ref, grads, acts):
    lane = lax.broadcasted_iota(jnp.int32, (BLK, VOX), 1)
    row, col = lane // COLS, lane % COLS
    for plane in range(PLANES):
        here = slice(plane * VOX, (plane + 1) * VOX)
        act = act_ref[plane]
        wide = act.astype(F32)
        acts[0:BLK, here] = jnp.where(col > 0, shifted(wide, -1, 1), 0.0).astype(BF16)
        acts[BLK : 2 * BLK, here] = act
        acts[2 * BLK : 3 * BLK, here] = jnp.where(
            col < COLS - 1, shifted(wide, 1, 1), 0.0
        ).astype(BF16)
        grad = grad_ref[plane]
        wide = grad.astype(F32)
        views = (
            jnp.where(row < ROWS - 1, shifted(wide, COLS, 1), 0.0).astype(BF16),
            grad,
            jnp.where(row > 0, shifted(wide, -COLS, 1), 0.0).astype(BF16),
        )
        for a in range(3):
            there = plane + a - 1
            if 0 <= there < PLANES:
                for b in range(3):
                    top = (a * 3 + b) * BLK
                    grads[top : top + BLK, there * VOX : (there + 1) * VOX] = views[b]
    blank = jnp.zeros((3 * BLK, VOX), BF16)
    grads[0 : 3 * BLK, (PLANES - 1) * VOX : PLANES * VOX] = blank
    grads[6 * BLK : 9 * BLK, 0:VOX] = blank
    total = lax.dot_general(
        grads[...], acts[...], (((1,), (1,)), ((), ())), preferred_element_type=F32
    )
    peak = jnp.max(jnp.abs(total), axis=0, keepdims=True)
    peak = jnp.max(peak, axis=1, keepdims=True)
    power = jnp.ceil(jnp.log2(jnp.maximum(peak, 2.0**-100)))
    total = total * jnp.exp2(TOP - power)
    tag = jnp.broadcast_to(power, (PIECE - DATA, 128))
    for part in range(4):
        pieces = [total[k * BLK + part * 16 : k * BLK + part * 16 + 16] for k in range(9)]
        block = jnp.concatenate(pieces, axis=0)
        tail = block[:, 128:192]
        tail = jnp.concatenate([tail[0:72], tail[72:144]], axis=1)
        lines = jnp.concatenate([block[:, 0:128], tail], axis=0)
        for half in range(2):
            for yl in range(2):
                start = (half * 2 + yl) * DATA
                dest = ((half * 2 + part // 2) * 2 + yl) * 2 + part % 2
                out_ref[dest] = jnp.concatenate([lines[start : start + DATA], tag], axis=0)


def weight_grads(given):
    return pl.pallas_call(
        weight_grad_kernel,
        out_shape=jax.ShapeDtypeStruct((32, PIECE, 128), F32),
        grid=(2,),
        in_specs=[
            pl.BlockSpec((PLANES, BLK, VOX), lambda i: (0, 2 * i, 0)),
            pl.BlockSpec((PLANES, BLK, VOX), lambda i: (0, 2 * i + 1, 0)),
        ],
        out_specs=pl.BlockSpec((16, PIECE, 128), lambda i: (i, 0, 0)),
        scratch_shapes=[
            pltpu.VMEM((9 * BLK, PLANES * VOX), BF16),
            pltpu.VMEM((3 * BLK, PLANES * VOX), BF16),
        ],
        compiler_params=PARAMS,
        cost_estimate=pl.CostEstimate(
            flops=4 * 27 * BLK * BLK * PLANES * VOX, bytes_accessed=4 * 1024 * 1024, transcendentals=0
        ),
        name="weight_grads",
    )(given, given)


def merge_kernel(parts_ref, out_ref):
    tags = [parts_ref[source, DATA : DATA + 1, 0:1] for source in range(32)]
    peak = tags[0]
    for tag in tags[1:]:
        peak = jnp.maximum(peak, tag)
    peak = peak + 3.0
    line = lax.broadcasted_iota(jnp.int32, (PIECE, 128), 0)
    for q in range(4):
        sources = [zl * 8 + (q // 2) * 4 + yl * 2 + q % 2 for zl in range(4) for yl in range(2)]
        total = jnp.zeros((PIECE, 128), F32)
        for source in sources:
            total = total + parts_ref[source] * jnp.exp2(tags[source] - peak)
        out_ref[q * PIECE : (q + 1) * PIECE] = jnp.where(line < DATA, total, peak)


def merge(parts):
    return pl.pallas_call(
        merge_kernel,
        out_shape=jax.ShapeDtypeStruct((4 * PIECE, 128), F32),
        in_specs=[VMEM],
        out_specs=VMEM,
        compiler_params=PARAMS,
        name="merge",
    )(parts)


def finish_kernel(sums_ref, out_ref):
    scales = [jnp.exp2(sums_ref[z, DATA : DATA + 1, 0:1] - TOP) for z in range(8)]
    for q in range(4):
        total = jnp.zeros((PIECE, 128), F32)
        for z in range(8):
            total = total + sums_ref[z, q * PIECE : (q + 1) * PIECE] * scales[z]
        total = total.astype(BF16)
        for dest in range(8):
            out_ref[dest, q] = total


def finish(sums):
    return pl.pallas_call(
        finish_kernel,
        out_shape=jax.ShapeDtypeStruct((8, 4, PIECE, 128), BF16),
        in_specs=[VMEM],
        out_specs=VMEM,
        compiler_params=PARAMS,
        name="finish",
    )(sums)


def unpack_kernel(pieces_ref, *out_refs):
    for which, out_ref in enumerate(out_refs):
        for pair in range(2):
            tiles = [
                jnp.concatenate(
                    [
                        pieces_ref[which * 4 + piece, 2 * pair + side].astype(F32)[0:DATA]
                        for piece in range(4)
                    ],
                    axis=0,
                )
                for side in range(2)
            ]
            tails = [
                jnp.concatenate([tile[144:LINES, 0:BLK], tile[144:LINES, BLK:128]], axis=0)
                for tile in tiles
            ]
            planes = (
                jnp.concatenate([tile[0:144, 0:BLK] for tile in tiles], axis=1),
                jnp.concatenate([tile[0:144, BLK:128] for tile in tiles], axis=1),
                jnp.concatenate(tails, axis=1),
            )
            for k in range(9):
                for c in range(3):
                    start = (3 * k + c) * CHANS + pair * 128
                    out_ref[:, start : start + 128] = planes[c][k * 16 : (k + 1) * 16]


def unpack(pieces):
    return pl.pallas_call(
        unpack_kernel,
        out_shape=[jax.ShapeDtypeStruct((16, 27 * CHANS), F32)] * 2,
        in_specs=[VMEM],
        out_specs=[VMEM] * 2,
        compiler_params=PARAMS,
        name="unpack",
    )(pieces)


def local(layer_input, hidden_pre, out_grad, weight_second):
    mp = ("x", "yh", "c")
    own = out_grad.reshape(ROWS, COLS, CHANS)
    pre = hidden_pre.reshape(ROWS, COLS, CHANS)
    first = layer_input.reshape(ROWS, COLS, CHANS)
    up = [(i, i + 1) for i in range(PLANES - 1)]
    low = lax.ppermute(own, mp, up)
    high = lax.ppermute(own, mp, [(b, a) for a, b in up])
    given = lax.all_to_all(
        front(low, own, high, pre, first, weight_second), mp, 0, 0, tiled=True
    )
    parts = weight_grads(given).astype(F16)
    parts = lax.all_to_all(parts, ("zl", "yh", "yl", "c"), 0, 0, tiled=True)
    mine = merge(parts.astype(F32)).astype(F16)
    sums = lax.all_gather(mine, "zh", axis=0, tiled=True).reshape(8, 4 * PIECE, 128)
    pieces = lax.all_to_all(finish(sums.astype(F32)), ("zl", "yl"), 0, 0, tiled=True)
    return tuple(unpack(pieces))


def solution(mesh):
    split = Mesh(mesh.devices.reshape(8, 4, 2, 4, 2, 2), ("zh", "zl", "yl", "x", "yh", "c"))
    dp, mp = ("zh", "zl", "yl"), ("x", "yh", "c")
    return jax.shard_map(
        local,
        mesh=split,
        in_specs=(P(dp, mp), P(dp, mp), P(dp, mp), P()),
        out_specs=(P(mp, None), P(mp, None)),
        check_vma=False,
    )
```

```python
import jax
import jax.numpy as jnp
from jax import lax
from jax.experimental import pallas as pl
from jax.experimental.pallas import tpu as pltpu
from jax.sharding import Mesh, PartitionSpec as P

F32 = jnp.float32
BF16 = jnp.bfloat16
F16 = jnp.float16
PLANES = 16
ROWS = 8
COLS = 32
VOX = ROWS * COLS
CHANS = 256
OUTS = 64
INS = 128
DATA = 54
PIECE = 56
TOP = 14.0

VMEM = pl.BlockSpec(memory_space=pltpu.VMEM)
PARAMS = pltpu.CompilerParams(vmem_limit_bytes=48 * 1024 * 1024)


def shifted(value, step, axis):
    size = value.shape[axis]
    return pltpu.roll(value, (-step) % size, axis)


def fill_views(plane, moved):
    col = lax.broadcasted_iota(jnp.int32, (VOX, CHANS), 0) % COLS
    blank = jnp.zeros((COLS, CHANS), BF16)
    wide = plane.astype(F32)
    views = (
        jnp.where(col < COLS - 1, shifted(wide, 1, 0), 0.0).astype(BF16),
        plane,
        jnp.where(col > 0, shifted(wide, -1, 0), 0.0).astype(BF16),
    )
    for c in range(3):
        moved[c, 0:COLS] = blank
        moved[c, COLS : COLS + VOX] = views[c]
        moved[c, COLS + VOX : 2 * COLS + VOX] = blank


def row_taps(total, moved, b, weight):
    start = (2 - b) * COLS
    for c in range(3):
        total = total + jnp.dot(
            moved[c, start : start + VOX],
            weight[:, c * CHANS : (c + 1) * CHANS],
            preferred_element_type=F32,
        )
    return total


def early_kernel(
    own_ref, pre_ref, first_ref, weight_ref, part_ref, kept_ref, turned_ref,
    planes, held, moved, plane_sems, held_sems, kept_sems,
):
    loads = [
        pltpu.make_async_copy(ref, planes.at[k], plane_sems.at[k])
        for k, ref in enumerate((own_ref, pre_ref, first_ref))
    ]

    def weights(part, target, sem):
        columns = pl.ds(part * 3 * CHANS, 3 * CHANS)
        return pltpu.make_async_copy(weight_ref.at[:, columns], target, sem)

    centre = [weights(3 + k, held.at[k], held_sems.at[k]) for k in range(3)]
    outer = [
        weights(part, kept_ref.at[k], kept_sems.at[k]) for k, part in enumerate((0, 1, 2, 6, 7, 8))
    ]
    for copy in loads + centre + outer:
        copy.start()
    loads[0].wait()
    own = planes[0].reshape(VOX, CHANS)
    fill_views(own, moved)
    total = jnp.zeros((VOX, CHANS), F32)
    for b in range(3):
        centre[b].wait()
        total = row_taps(total, moved, b, held.at[b])
    part_ref[...] = total
    turned_ref[0] = own.T
    loads[1].wait()
    turned_ref[1] = jnp.maximum(planes[1].reshape(VOX, CHANS), 0).T
    loads[2].wait()
    turned_ref[2] = planes[2].reshape(VOX, CHANS).T
    for copy in outer:
        copy.wait()


def early(own, pre, first, weight):
    return pl.pallas_call(
        early_kernel,
        out_shape=[
            jax.ShapeDtypeStruct((VOX, CHANS), F32),
            jax.ShapeDtypeStruct((6, CHANS, 3 * CHANS), BF16),
            jax.ShapeDtypeStruct((3, CHANS, VOX), BF16),
        ],
        in_specs=[pl.BlockSpec(memory_space=pltpu.HBM)] * 4,
        out_specs=[VMEM] * 3,
        scratch_shapes=[
            pltpu.VMEM((3, ROWS, COLS, CHANS), BF16),
            pltpu.VMEM((3, CHANS, 3 * CHANS), BF16),
            pltpu.VMEM((3, VOX + 2 * COLS, CHANS), BF16),
            pltpu.SemaphoreType.DMA((3,)),
            pltpu.SemaphoreType.DMA((3,)),
            pltpu.SemaphoreType.DMA((6,)),
        ],
        compiler_params=PARAMS,
        cost_estimate=pl.CostEstimate(
            flops=2 * VOX * 9 * CHANS * CHANS, bytes_accessed=5 * 1024 * 1024, transcendentals=0
        ),
        name="early",
    )(own, pre, first, weight)


def late_kernel(low_ref, high_ref, part_ref, kept_ref, turned_ref, out_ref, moved):
    total = part_ref[...]
    for side, source in enumerate((high_ref, low_ref)):
        fill_views(source[...].reshape(VOX, CHANS), moved.at[side])
        for b in range(3):
            total = row_taps(total, moved.at[side], b, kept_ref.at[side * 3 + b])
    second = turned_ref[1]
    hidden = jnp.where(second > 0, total.T, 0.0).astype(BF16)
    grad, first = turned_ref[0], turned_ref[2]
    for x in range(4):
        for yh in range(2):
            dest = (x * 2 + yh) * 2
            for c, (left, right) in enumerate(((grad, second), (hidden, first))):
                out_ref[dest + c, 0:OUTS] = left[OUTS * x : OUTS * (x + 1)]
                out_ref[dest + c, OUTS : OUTS + INS] = right[INS * yh : INS * (yh + 1)]


def late(low, high, part, kept, turned):
    return pl.pallas_call(
        late_kernel,
        out_shape=jax.ShapeDtypeStruct((PLANES, OUTS + INS, VOX), BF16),
        in_specs=[VMEM] * 5,
        out_specs=VMEM,
        scratch_shapes=[pltpu.VMEM((2, 3, VOX + 2 * COLS, CHANS), BF16)],
        compiler_params=PARAMS,
        cost_estimate=pl.CostEstimate(
            flops=2 * VOX * 18 * CHANS * CHANS, bytes_accessed=3 * 1024 * 1024, transcendentals=0
        ),
        name="late",
    )(low, high, part, kept, turned)


def weight_grad_kernel(given_ref, out_ref, grads, acts):
    col = lax.broadcasted_iota(jnp.int32, (INS, VOX), 1) % COLS
    row = lax.broadcasted_iota(jnp.int32, (OUTS, VOX), 1) // COLS
    for plane in range(PLANES):
        here = slice(plane * VOX, (plane + 1) * VOX)
        act = given_ref[plane, OUTS : OUTS + INS]
        wide = act.astype(F32)
        acts[0:INS, here] = jnp.where(col > 0, shifted(wide, -1, 1), 0.0).astype(BF16)
        acts[INS : 2 * INS, here] = act
        acts[2 * INS : 3 * INS, here] = jnp.where(
            col < COLS - 1, shifted(wide, 1, 1), 0.0
        ).astype(BF16)
        grad = given_ref[plane, 0:OUTS]
        wide = grad.astype(F32)
        views = (
            jnp.where(row < ROWS - 1, shifted(wide, COLS, 1), 0.0).astype(BF16),
            grad,
            jnp.where(row > 0, shifted(wide, -COLS, 1), 0.0).astype(BF16),
        )
        for a in range(3):
            there = plane + a - 1
            if 0 <= there < PLANES:
                for b in range(3):
                    top = (a * 3 + b) * OUTS
                    grads[top : top + OUTS, there * VOX : (there + 1) * VOX] = views[b]
    blank = jnp.zeros((3 * OUTS, VOX), BF16)
    grads[0 : 3 * OUTS, (PLANES - 1) * VOX : PLANES * VOX] = blank
    grads[6 * OUTS : 9 * OUTS, 0:VOX] = blank
    total = lax.dot_general(
        grads[...], acts[...], (((1,), (1,)), ((), ())), preferred_element_type=F32
    )
    peak = jnp.max(jnp.abs(total), axis=0, keepdims=True)
    peak = jnp.max(peak, axis=1, keepdims=True)
    power = jnp.ceil(jnp.log2(jnp.maximum(peak, 2.0**-100)))
    total = total * jnp.exp2(TOP - power)
    tag = jnp.broadcast_to(power, (PIECE - DATA, 128))
    for part in range(4):
        lines = jnp.concatenate(
            [
                total[k * OUTS + part * 16 : k * OUTS + part * 16 + 16, c * INS : (c + 1) * INS]
                for k in range(9)
                for c in range(3)
            ],
            axis=0,
        )
        for zl in range(4):
            for yl in range(2):
                start = (zl * 2 + yl) * DATA
                dest = ((zl * 2 + part // 2) * 2 + yl) * 2 + part % 2
                out_ref[dest] = jnp.concatenate([lines[start : start + DATA], tag], axis=0)


def weight_grad(given):
    return pl.pallas_call(
        weight_grad_kernel,
        out_shape=jax.ShapeDtypeStruct((32, PIECE, 128), F32),
        in_specs=[VMEM],
        out_specs=VMEM,
        scratch_shapes=[
            pltpu.VMEM((9 * OUTS, PLANES * VOX), BF16),
            pltpu.VMEM((3 * INS, PLANES * VOX), BF16),
        ],
        compiler_params=PARAMS,
        cost_estimate=pl.CostEstimate(
            flops=2 * 27 * OUTS * INS * PLANES * VOX, bytes_accessed=4 * 1024 * 1024, transcendentals=0
        ),
        name="weight_grad",
    )(given)


def merge_kernel(parts_ref, out_ref):
    tags = [parts_ref[source, DATA : DATA + 1, 0:1] for source in range(32)]
    peak = tags[0]
    for tag in tags[1:]:
        peak = jnp.maximum(peak, tag)
    peak = peak + 3.0
    line = lax.broadcasted_iota(jnp.int32, (PIECE, 128), 0)
    for q in range(4):
        sources = [zl * 8 + (q // 2) * 4 + yl * 2 + q % 2 for zl in range(4) for yl in range(2)]
        total = jnp.zeros((PIECE, 128), F32)
        for source in sources:
            total = total + parts_ref[source] * jnp.exp2(tags[source] - peak)
        out_ref[q * PIECE : (q + 1) * PIECE] = jnp.where(line < DATA, total, peak)


def merge(parts):
    return pl.pallas_call(
        merge_kernel,
        out_shape=jax.ShapeDtypeStruct((4 * PIECE, 128), F32),
        in_specs=[VMEM],
        out_specs=VMEM,
        compiler_params=PARAMS,
        name="merge",
    )(parts)


def finish_kernel(sums_ref, out_ref):
    scales = [jnp.exp2(sums_ref[z, DATA : DATA + 1, 0:1] - TOP) for z in range(8)]
    for q in range(4):
        total = jnp.zeros((PIECE, 128), F32)
        for z in range(8):
            total = total + sums_ref[z, q * PIECE : (q + 1) * PIECE] * scales[z]
        total = total.astype(BF16)
        for dest in range(8):
            out_ref[dest, q] = total


def finish(sums):
    return pl.pallas_call(
        finish_kernel,
        out_shape=jax.ShapeDtypeStruct((8, 4, PIECE, 128), BF16),
        in_specs=[VMEM],
        out_specs=VMEM,
        compiler_params=PARAMS,
        name="finish",
    )(sums)


def unpack_kernel(pieces_ref, *out_refs):
    for c, out_ref in enumerate(out_refs):
        for yh in range(2):
            lines = jnp.concatenate(
                [pieces_ref[piece, yh * 2 + c].astype(F32)[0:DATA] for piece in range(8)], axis=0
            )
            for tap in range(27):
                start = tap * CHANS + yh * INS
                out_ref[:, start : start + INS] = lines[tap * 16 : (tap + 1) * 16]


def unpack(pieces):
    return pl.pallas_call(
        unpack_kernel,
        out_shape=[jax.ShapeDtypeStruct((16, 27 * CHANS), F32)] * 2,
        in_specs=[VMEM],
        out_specs=[VMEM] * 2,
        compiler_params=PARAMS,
        name="unpack",
    )(pieces)


def local(layer_input, hidden_pre, out_grad, weight_second):
    mp = ("x", "yh", "c")
    own = out_grad.reshape(ROWS, COLS, CHANS)
    pre = hidden_pre.reshape(ROWS, COLS, CHANS)
    first = layer_input.reshape(ROWS, COLS, CHANS)
    up = [(i, i + 1) for i in range(PLANES - 1)]
    low = lax.ppermute(own, mp, up)
    high = lax.ppermute(own, mp, [(b, a) for a, b in up])
    kept = [pltpu.with_memory_space_constraint(a, pltpu.HBM) for a in (own, pre, first)]
    given = late(low, high, *early(*kept, weight_second))
    given = lax.all_to_all(given, mp, 0, 0, tiled=True)
    parts = weight_grad(given).astype(F16)
    parts = lax.all_to_all(parts, ("zl", "yh", "yl", "c"), 0, 0, tiled=True)
    mine = merge(parts.astype(F32)).astype(F16)
    sums = lax.all_gather(mine, "zh", axis=0, tiled=True).reshape(8, 4 * PIECE, 128)
    pieces = lax.all_to_all(finish(sums.astype(F32)), ("zl", "yl"), 0, 0, tiled=True)
    return tuple(unpack(pieces))


def solution(mesh):
    split = Mesh(mesh.devices.reshape(8, 4, 2, 4, 2, 2), ("zh", "zl", "yl", "x", "yh", "c"))
    dp, mp = ("zh", "zl", "yl"), ("x", "yh", "c")
    return jax.shard_map(
        local,
        mesh=split,
        in_specs=(P(dp, mp), P(dp, mp), P(dp, mp), P()),
        out_specs=(P(mp, None), P(mp, None)),
        check_vma=False,
    )
```

```python
import jax
import jax.numpy as jnp
from jax import lax
from jax.experimental import pallas as pl
from jax.experimental.pallas import tpu as pltpu
from jax.sharding import Mesh, PartitionSpec as P

F32 = jnp.float32
BF16 = jnp.bfloat16
F16 = jnp.float16
PLANES = 16
ROWS = 8
COLS = 32
VOX = ROWS * COLS
CHANS = 256
OUTS = 64
INS = 128
DATA = 54
PIECE = 56
TOP = 14.0

VMEM = pl.BlockSpec(memory_space=pltpu.VMEM)
PARAMS = pltpu.CompilerParams(vmem_limit_bytes=48 * 1024 * 1024)


def shifted(value, step, axis):
    size = value.shape[axis]
    return pltpu.roll(value, (-step) % size, axis)


def fill_views(plane, moved):
    col = lax.broadcasted_iota(jnp.int32, (VOX, CHANS), 0) % COLS
    blank = jnp.zeros((COLS, CHANS), BF16)
    wide = plane.astype(F32)
    views = (
        jnp.where(col < COLS - 1, shifted(wide, 1, 0), 0.0).astype(BF16),
        plane,
        jnp.where(col > 0, shifted(wide, -1, 0), 0.0).astype(BF16),
    )
    for c in range(3):
        moved[c, 0:COLS] = blank
        moved[c, COLS : COLS + VOX] = views[c]
        moved[c, COLS + VOX : 2 * COLS + VOX] = blank


def row_taps(total, moved, b, weight):
    start = (2 - b) * COLS
    for c in range(3):
        total = total + jnp.dot(
            moved[c, start : start + VOX],
            weight[:, c * CHANS : (c + 1) * CHANS],
            preferred_element_type=F32,
        )
    return total


def early_kernel(
    own_ref, pre_ref, first_ref, weight_ref, part_ref, kept_ref, turned_ref,
    planes, held, moved, plane_sems, held_sems, kept_sems,
):
    loads = [
        pltpu.make_async_copy(ref, planes.at[k], plane_sems.at[k])
        for k, ref in enumerate((own_ref, pre_ref, first_ref))
    ]

    def weights(part, target, sem):
        columns = pl.ds(part * 3 * CHANS, 3 * CHANS)
        return pltpu.make_async_copy(weight_ref.at[:, columns], target, sem)

    centre = [weights(3 + k, held.at[k], held_sems.at[k]) for k in range(3)]
    outer = [
        weights(part, kept_ref.at[k], kept_sems.at[k]) for k, part in enumerate((0, 1, 2, 6, 7, 8))
    ]
    for copy in loads + centre + outer:
        copy.start()
    loads[0].wait()
    own = planes[0].reshape(VOX, CHANS)
    fill_views(own, moved)
    total = jnp.zeros((VOX, CHANS), F32)
    for b in range(3):
        centre[b].wait()
        total = row_taps(total, moved, b, held.at[b])
    part_ref[...] = total
    turned_ref[0] = own.T
    loads[1].wait()
    turned_ref[1] = jnp.maximum(planes[1].reshape(VOX, CHANS), 0).T
    loads[2].wait()
    turned_ref[2] = planes[2].reshape(VOX, CHANS).T
    for copy in outer:
        copy.wait()


def early(own, pre, first, weight):
    return pl.pallas_call(
        early_kernel,
        out_shape=[
            jax.ShapeDtypeStruct((VOX, CHANS), F32),
            jax.ShapeDtypeStruct((6, CHANS, 3 * CHANS), BF16),
            jax.ShapeDtypeStruct((3, CHANS, VOX), BF16),
        ],
        in_specs=[pl.BlockSpec(memory_space=pltpu.HBM)] * 4,
        out_specs=[VMEM] * 3,
        scratch_shapes=[
            pltpu.VMEM((3, ROWS, COLS, CHANS), BF16),
            pltpu.VMEM((3, CHANS, 3 * CHANS), BF16),
            pltpu.VMEM((3, VOX + 2 * COLS, CHANS), BF16),
            pltpu.SemaphoreType.DMA((3,)),
            pltpu.SemaphoreType.DMA((3,)),
            pltpu.SemaphoreType.DMA((6,)),
        ],
        compiler_params=PARAMS,
        cost_estimate=pl.CostEstimate(
            flops=2 * VOX * 9 * CHANS * CHANS, bytes_accessed=5 * 1024 * 1024, transcendentals=0
        ),
        name="early",
    )(own, pre, first, weight)


def late_kernel(core_ref, near_ref, far_ref, part_ref, kept_ref, turned_ref, out_ref, moved):
    core = core_ref[0]
    total = part_ref[...]
    for side, (source, taps) in enumerate(((near_ref, core), (far_ref, 1 - core))):
        fill_views(source[...].reshape(VOX, CHANS), moved.at[side])
        for b in range(3):
            total = row_taps(total, moved.at[side], b, kept_ref.at[taps * 3 + b])
    second = turned_ref[1]
    hidden = jnp.where(second > 0, total.T, 0.0).astype(BF16)
    grad, first = turned_ref[0], turned_ref[2]
    for x in range(4):
        for yh in range(2):
            dest = (x * 2 + yh) * 2
            for c, (left, right) in enumerate(((grad, second), (hidden, first))):
                out_ref[dest + c, 0:OUTS] = left[OUTS * x : OUTS * (x + 1)]
                out_ref[dest + c, OUTS : OUTS + INS] = right[INS * yh : INS * (yh + 1)]


def late(core, near, far, part, kept, turned):
    return pl.pallas_call(
        late_kernel,
        out_shape=jax.ShapeDtypeStruct((PLANES, OUTS + INS, VOX), BF16),
        in_specs=[pl.BlockSpec(memory_space=pltpu.SMEM)] + [VMEM] * 5,
        out_specs=VMEM,
        scratch_shapes=[pltpu.VMEM((2, 3, VOX + 2 * COLS, CHANS), BF16)],
        compiler_params=PARAMS,
        cost_estimate=pl.CostEstimate(
            flops=2 * VOX * 18 * CHANS * CHANS, bytes_accessed=3 * 1024 * 1024, transcendentals=0
        ),
        name="late",
    )(core, near, far, part, kept, turned)


def weight_grad_kernel(given_ref, out_ref, grads, acts):
    col = lax.broadcasted_iota(jnp.int32, (INS, VOX), 1) % COLS
    row = lax.broadcasted_iota(jnp.int32, (OUTS, VOX), 1) // COLS
    for plane in range(PLANES):
        here = slice(plane * VOX, (plane + 1) * VOX)
        act = given_ref[plane, OUTS : OUTS + INS]
        wide = act.astype(F32)
        acts[0:INS, here] = jnp.where(col > 0, shifted(wide, -1, 1), 0.0).astype(BF16)
        acts[INS : 2 * INS, here] = act
        acts[2 * INS : 3 * INS, here] = jnp.where(
            col < COLS - 1, shifted(wide, 1, 1), 0.0
        ).astype(BF16)
        grad = given_ref[plane, 0:OUTS]
        wide = grad.astype(F32)
        views = (
            jnp.where(row < ROWS - 1, shifted(wide, COLS, 1), 0.0).astype(BF16),
            grad,
            jnp.where(row > 0, shifted(wide, -COLS, 1), 0.0).astype(BF16),
        )
        for a in range(3):
            there = plane + a - 1
            if 0 <= there < PLANES:
                for b in range(3):
                    top = (a * 3 + b) * OUTS
                    grads[top : top + OUTS, there * VOX : (there + 1) * VOX] = views[b]
    blank = jnp.zeros((3 * OUTS, VOX), BF16)
    grads[0 : 3 * OUTS, (PLANES - 1) * VOX : PLANES * VOX] = blank
    grads[6 * OUTS : 9 * OUTS, 0:VOX] = blank
    total = lax.dot_general(
        grads[...], acts[...], (((1,), (1,)), ((), ())), preferred_element_type=F32
    )
    peak = jnp.max(jnp.abs(total), axis=0, keepdims=True)
    peak = jnp.max(peak, axis=1, keepdims=True)
    power = jnp.ceil(jnp.log2(jnp.maximum(peak, 2.0**-100)))
    total = total * jnp.exp2(TOP - power)
    tag = jnp.broadcast_to(power, (PIECE - DATA, 128))
    for part in range(4):
        lines = jnp.concatenate(
            [
                total[k * OUTS + part * 16 : k * OUTS + part * 16 + 16, c * INS : (c + 1) * INS]
                for k in range(9)
                for c in range(3)
            ],
            axis=0,
        )
        for zl in range(4):
            for yl in range(2):
                start = (zl * 2 + yl) * DATA
                dest = ((zl * 2 + part // 2) * 2 + yl) * 2 + part % 2
                out_ref[dest] = jnp.concatenate([lines[start : start + DATA], tag], axis=0)


def weight_grad(given):
    return pl.pallas_call(
        weight_grad_kernel,
        out_shape=jax.ShapeDtypeStruct((32, PIECE, 128), F32),
        in_specs=[VMEM],
        out_specs=VMEM,
        scratch_shapes=[
            pltpu.VMEM((9 * OUTS, PLANES * VOX), BF16),
            pltpu.VMEM((3 * INS, PLANES * VOX), BF16),
        ],
        compiler_params=PARAMS,
        cost_estimate=pl.CostEstimate(
            flops=2 * 27 * OUTS * INS * PLANES * VOX, bytes_accessed=4 * 1024 * 1024, transcendentals=0
        ),
        name="weight_grad",
    )(given)


def merge_kernel(parts_ref, out_ref):
    tags = [parts_ref[source, DATA : DATA + 1, 0:1] for source in range(32)]
    peak = tags[0]
    for tag in tags[1:]:
        peak = jnp.maximum(peak, tag)
    peak = peak + 3.0
    line = lax.broadcasted_iota(jnp.int32, (PIECE, 128), 0)
    for q in range(4):
        sources = [zl * 8 + (q // 2) * 4 + yl * 2 + q % 2 for zl in range(4) for yl in range(2)]
        total = jnp.zeros((PIECE, 128), F32)
        for source in sources:
            total = total + parts_ref[source] * jnp.exp2(tags[source] - peak)
        out_ref[q * PIECE : (q + 1) * PIECE] = jnp.where(line < DATA, total, peak)


def merge(parts):
    return pl.pallas_call(
        merge_kernel,
        out_shape=jax.ShapeDtypeStruct((4 * PIECE, 128), F32),
        in_specs=[VMEM],
        out_specs=VMEM,
        compiler_params=PARAMS,
        name="merge",
    )(parts)


def finish_kernel(sums_ref, out_ref):
    scales = [jnp.exp2(sums_ref[z, DATA : DATA + 1, 0:1] - TOP) for z in range(8)]
    for q in range(4):
        total = jnp.zeros((PIECE, 128), F32)
        for z in range(8):
            total = total + sums_ref[z, q * PIECE : (q + 1) * PIECE] * scales[z]
        total = total.astype(BF16)
        for dest in range(8):
            out_ref[dest, q] = total


def finish(sums):
    return pl.pallas_call(
        finish_kernel,
        out_shape=jax.ShapeDtypeStruct((8, 4, PIECE, 128), BF16),
        in_specs=[VMEM],
        out_specs=VMEM,
        compiler_params=PARAMS,
        name="finish",
    )(sums)


def unpack_kernel(pieces_ref, *out_refs):
    for c, out_ref in enumerate(out_refs):
        for yh in range(2):
            lines = jnp.concatenate(
                [pieces_ref[piece, yh * 2 + c].astype(F32)[0:DATA] for piece in range(8)], axis=0
            )
            for tap in range(27):
                start = tap * CHANS + yh * INS
                out_ref[:, start : start + INS] = lines[tap * 16 : (tap + 1) * 16]


def unpack(pieces):
    return pl.pallas_call(
        unpack_kernel,
        out_shape=[jax.ShapeDtypeStruct((16, 27 * CHANS), F32)] * 2,
        in_specs=[VMEM],
        out_specs=[VMEM] * 2,
        compiler_params=PARAMS,
        name="unpack",
    )(pieces)


def local(layer_input, hidden_pre, out_grad, weight_second):
    mp = ("x", "yh", "c")
    own = out_grad.reshape(ROWS, COLS, CHANS)
    pre = hidden_pre.reshape(ROWS, COLS, CHANS)
    first = layer_input.reshape(ROWS, COLS, CHANS)
    near = lax.ppermute(own, mp, [(i, i ^ 1) for i in range(PLANES)])
    far = lax.ppermute(own, mp, [(i, i + (1 if i % 2 else -1)) for i in range(1, PLANES - 1)])
    core = lax.axis_index("c").reshape(1)
    kept = [pltpu.with_memory_space_constraint(a, pltpu.HBM) for a in (own, pre, first)]
    given = late(core, near, far, *early(*kept, weight_second))
    given = lax.all_to_all(given, mp, 0, 0, tiled=True)
    parts = weight_grad(given).astype(F16)
    parts = lax.all_to_all(parts, ("zl", "yh", "yl", "c"), 0, 0, tiled=True)
    mine = merge(parts.astype(F32)).astype(F16)
    sums = lax.all_gather(mine, "zh", axis=0, tiled=True).reshape(8, 4 * PIECE, 128)
    pieces = lax.all_to_all(finish(sums.astype(F32)), ("zl", "yl"), 0, 0, tiled=True)
    return tuple(unpack(pieces))


def solution(mesh):
    split = Mesh(mesh.devices.reshape(8, 4, 2, 4, 2, 2), ("zh", "zl", "yl", "x", "yh", "c"))
    dp, mp = ("zh", "zl", "yl"), ("x", "yh", "c")
    return jax.shard_map(
        local,
        mesh=split,
        in_specs=(P(dp, mp), P(dp, mp), P(dp, mp), P()),
        out_specs=(P(mp, None), P(mp, None)),
        check_vma=False,
    )
```

```python
import jax
import jax.numpy as jnp
from jax import lax
from jax.experimental import pallas as pl
from jax.experimental.pallas import tpu as pltpu
from jax.sharding import Mesh, PartitionSpec as P

F32 = jnp.float32
BF16 = jnp.bfloat16
F16 = jnp.float16
PLANES = 16
HALF = PLANES // 2
ROWS = 8
COLS = 32
VOX = ROWS * COLS
CHANS = 256
OUTS = 64
INS = 128
DATA = 54
PIECE = 56
TOP = 14.0

VMEM = pl.BlockSpec(memory_space=pltpu.VMEM)
PARAMS = pltpu.CompilerParams(vmem_limit_bytes=48 * 1024 * 1024)


def shifted(value, step, axis):
    size = value.shape[axis]
    return pltpu.roll(value, (-step) % size, axis)


def fill_views(plane, moved):
    col = lax.broadcasted_iota(jnp.int32, (VOX, CHANS), 0) % COLS
    blank = jnp.zeros((COLS, CHANS), BF16)
    wide = plane.astype(F32)
    views = (
        jnp.where(col < COLS - 1, shifted(wide, 1, 0), 0.0).astype(BF16),
        plane,
        jnp.where(col > 0, shifted(wide, -1, 0), 0.0).astype(BF16),
    )
    for c in range(3):
        moved[c, 0:COLS] = blank
        moved[c, COLS : COLS + VOX] = views[c]
        moved[c, COLS + VOX : 2 * COLS + VOX] = blank


def row_taps(total, moved, b, weight):
    start = (2 - b) * COLS
    for c in range(3):
        total = total + jnp.dot(
            moved[c, start : start + VOX],
            weight[:, c * CHANS : (c + 1) * CHANS],
            preferred_element_type=F32,
        )
    return total


def early_kernel(
    own_ref, pre_ref, first_ref, weight_ref, part_ref, kept_ref, turned_ref,
    planes, held, moved, plane_sems, held_sems, kept_sems,
):
    loads = [
        pltpu.make_async_copy(ref, planes.at[k], plane_sems.at[k])
        for k, ref in enumerate((own_ref, pre_ref, first_ref))
    ]

    def weights(part, target, sem):
        columns = pl.ds(part * 3 * CHANS, 3 * CHANS)
        return pltpu.make_async_copy(weight_ref.at[:, columns], target, sem)

    centre = [weights(3 + k, held.at[k], held_sems.at[k]) for k in range(3)]
    outer = [
        weights(part, kept_ref.at[k], kept_sems.at[k]) for k, part in enumerate((0, 1, 2, 6, 7, 8))
    ]
    for copy in loads + centre + outer:
        copy.start()
    loads[0].wait()
    own = planes[0].reshape(VOX, CHANS)
    fill_views(own, moved)
    total = jnp.zeros((VOX, CHANS), F32)
    for b in range(3):
        centre[b].wait()
        total = row_taps(total, moved, b, held.at[b])
    part_ref[...] = total
    turned_ref[0] = own.T
    loads[1].wait()
    turned_ref[1] = jnp.maximum(planes[1].reshape(VOX, CHANS), 0).T
    loads[2].wait()
    turned_ref[2] = planes[2].reshape(VOX, CHANS).T
    for copy in outer:
        copy.wait()


def early(own, pre, first, weight):
    return pl.pallas_call(
        early_kernel,
        out_shape=[
            jax.ShapeDtypeStruct((VOX, CHANS), F32),
            jax.ShapeDtypeStruct((6, CHANS, 3 * CHANS), BF16),
            jax.ShapeDtypeStruct((3, CHANS, VOX), BF16),
        ],
        in_specs=[pl.BlockSpec(memory_space=pltpu.HBM)] * 4,
        out_specs=[VMEM] * 3,
        scratch_shapes=[
            pltpu.VMEM((3, ROWS, COLS, CHANS), BF16),
            pltpu.VMEM((3, CHANS, 3 * CHANS), BF16),
            pltpu.VMEM((3, VOX + 2 * COLS, CHANS), BF16),
            pltpu.SemaphoreType.DMA((3,)),
            pltpu.SemaphoreType.DMA((3,)),
            pltpu.SemaphoreType.DMA((6,)),
        ],
        compiler_params=PARAMS,
        cost_estimate=pl.CostEstimate(
            flops=2 * VOX * 9 * CHANS * CHANS, bytes_accessed=5 * 1024 * 1024, transcendentals=0
        ),
        name="early",
    )(own, pre, first, weight)


def late_kernel(core_ref, near_ref, far_ref, part_ref, kept_ref, turned_ref, out_ref, moved):
    core = core_ref[0]
    total = part_ref[...]
    for side, (source, taps) in enumerate(((near_ref, core), (far_ref, 1 - core))):
        fill_views(source[...].reshape(VOX, CHANS), moved.at[side])
        for b in range(3):
            total = row_taps(total, moved.at[side], b, kept_ref.at[taps * 3 + b])
    second = turned_ref[1]
    hidden = jnp.where(second > 0, total.T, 0.0).astype(BF16)
    grad, first = turned_ref[0], turned_ref[2]
    for x in range(4):
        for yh in range(2):
            dest = (x * 2 + yh) * 2
            for c, (left, right) in enumerate(((grad, second), (hidden, first))):
                out_ref[dest + c, 0:OUTS] = left[OUTS * x : OUTS * (x + 1)]
                out_ref[dest + c, OUTS : OUTS + INS] = right[INS * yh : INS * (yh + 1)]


def late(core, near, far, part, kept, turned):
    return pl.pallas_call(
        late_kernel,
        out_shape=jax.ShapeDtypeStruct((PLANES, OUTS + INS, VOX), BF16),
        in_specs=[pl.BlockSpec(memory_space=pltpu.SMEM)] + [VMEM] * 5,
        out_specs=VMEM,
        scratch_shapes=[pltpu.VMEM((2, 3, VOX + 2 * COLS, CHANS), BF16)],
        compiler_params=PARAMS,
        cost_estimate=pl.CostEstimate(
            flops=2 * VOX * 18 * CHANS * CHANS, bytes_accessed=3 * 1024 * 1024, transcendentals=0
        ),
        name="late",
    )(core, near, far, part, kept, turned)


def weight_grad_kernel(given_ref, out_ref, grads_low, grads_high, acts_low, acts_high):
    all_grads, all_acts = (grads_low, grads_high), (acts_low, acts_high)
    blank = jnp.zeros((3 * OUTS, VOX), BF16)
    grads_high[0 : 3 * OUTS, (HALF - 1) * VOX : HALF * VOX] = blank
    grads_low[6 * OUTS : 9 * OUTS, 0:VOX] = blank
    total = None
    col = lax.broadcasted_iota(jnp.int32, (INS, VOX), 1) % COLS
    row = lax.broadcasted_iota(jnp.int32, (OUTS, VOX), 1) // COLS
    for plane in range(PLANES):
        here = slice(plane % HALF * VOX, (plane % HALF + 1) * VOX)
        acts = all_acts[plane // HALF]
        act = given_ref[plane, OUTS : OUTS + INS]
        wide = act.astype(F32)
        acts[0:INS, here] = jnp.where(col > 0, shifted(wide, -1, 1), 0.0).astype(BF16)
        acts[INS : 2 * INS, here] = act
        acts[2 * INS : 3 * INS, here] = jnp.where(
            col < COLS - 1, shifted(wide, 1, 1), 0.0
        ).astype(BF16)
        grad = given_ref[plane, 0:OUTS]
        wide = grad.astype(F32)
        views = (
            jnp.where(row < ROWS - 1, shifted(wide, COLS, 1), 0.0).astype(BF16),
            grad,
            jnp.where(row > 0, shifted(wide, -COLS, 1), 0.0).astype(BF16),
        )
        for a in range(3):
            there = plane + a - 1
            if 0 <= there < PLANES:
                start = there % HALF * VOX
                for b in range(3):
                    top = (a * 3 + b) * OUTS
                    all_grads[there // HALF][top : top + OUTS, start : start + VOX] = views[b]
        if plane in (HALF, PLANES - 1):
            half = 0 if plane == HALF else 1
            term = lax.dot_general(
                all_grads[half][...],
                all_acts[half][...],
                (((1,), (1,)), ((), ())),
                preferred_element_type=F32,
            )
            total = term if total is None else total + term
    peak = jnp.max(jnp.abs(total), axis=0, keepdims=True)
    peak = jnp.max(peak, axis=1, keepdims=True)
    power = jnp.ceil(jnp.log2(jnp.maximum(peak, 2.0**-100)))
    total = total * jnp.exp2(TOP - power)
    tag = jnp.broadcast_to(power, (PIECE - DATA, 128))
    for part in range(4):
        lines = jnp.concatenate(
            [
                total[k * OUTS + part * 16 : k * OUTS + part * 16 + 16, c * INS : (c + 1) * INS]
                for k in range(9)
                for c in range(3)
            ],
            axis=0,
        )
        for zl in range(4):
            for yl in range(2):
                start = (zl * 2 + yl) * DATA
                dest = ((zl * 2 + part // 2) * 2 + yl) * 2 + part % 2
                out_ref[dest] = jnp.concatenate([lines[start : start + DATA], tag], axis=0)


def weight_grad(given):
    return pl.pallas_call(
        weight_grad_kernel,
        out_shape=jax.ShapeDtypeStruct((32, PIECE, 128), F32),
        in_specs=[VMEM],
        out_specs=VMEM,
        scratch_shapes=[
            pltpu.VMEM((9 * OUTS, HALF * VOX), BF16),
            pltpu.VMEM((9 * OUTS, HALF * VOX), BF16),
            pltpu.VMEM((3 * INS, HALF * VOX), BF16),
            pltpu.VMEM((3 * INS, HALF * VOX), BF16),
        ],
        compiler_params=PARAMS,
        cost_estimate=pl.CostEstimate(
            flops=2 * 27 * OUTS * INS * PLANES * VOX, bytes_accessed=4 * 1024 * 1024, transcendentals=0
        ),
        name="weight_grad",
    )(given)


def merge_kernel(parts_ref, out_ref):
    tags = [parts_ref[source, DATA : DATA + 1, 0:1] for source in range(32)]
    peak = tags[0]
    for tag in tags[1:]:
        peak = jnp.maximum(peak, tag)
    peak = peak + 3.0
    line = lax.broadcasted_iota(jnp.int32, (PIECE, 128), 0)
    for q in range(4):
        sources = [zl * 8 + (q // 2) * 4 + yl * 2 + q % 2 for zl in range(4) for yl in range(2)]
        total = jnp.zeros((PIECE, 128), F32)
        for source in sources:
            total = total + parts_ref[source] * jnp.exp2(tags[source] - peak)
        out_ref[q * PIECE : (q + 1) * PIECE] = jnp.where(line < DATA, total, peak)


def merge(parts):
    return pl.pallas_call(
        merge_kernel,
        out_shape=jax.ShapeDtypeStruct((4 * PIECE, 128), F32),
        in_specs=[VMEM],
        out_specs=VMEM,
        compiler_params=PARAMS,
        name="merge",
    )(parts)


def finish_kernel(sums_ref, out_ref):
    scales = [jnp.exp2(sums_ref[z, DATA : DATA + 1, 0:1] - TOP) for z in range(8)]
    for q in range(4):
        total = jnp.zeros((PIECE, 128), F32)
        for z in range(8):
            total = total + sums_ref[z, q * PIECE : (q + 1) * PIECE] * scales[z]
        total = total.astype(BF16)
        for dest in range(8):
            out_ref[dest, q] = total


def finish(sums):
    return pl.pallas_call(
        finish_kernel,
        out_shape=jax.ShapeDtypeStruct((8, 4, PIECE, 128), BF16),
        in_specs=[VMEM],
        out_specs=VMEM,
        compiler_params=PARAMS,
        name="finish",
    )(sums)


def unpack_kernel(pieces_ref, *out_refs):
    for c, out_ref in enumerate(out_refs):
        for yh in range(2):
            lines = jnp.concatenate(
                [pieces_ref[piece, yh * 2 + c].astype(F32)[0:DATA] for piece in range(8)], axis=0
            )
            for tap in range(27):
                start = tap * CHANS + yh * INS
                out_ref[:, start : start + INS] = lines[tap * 16 : (tap + 1) * 16]


def unpack(pieces):
    return pl.pallas_call(
        unpack_kernel,
        out_shape=[jax.ShapeDtypeStruct((16, 27 * CHANS), F32)] * 2,
        in_specs=[VMEM],
        out_specs=[VMEM] * 2,
        compiler_params=PARAMS,
        name="unpack",
    )(pieces)


def local(layer_input, hidden_pre, out_grad, weight_second):
    mp = ("x", "yh", "c")
    own = out_grad.reshape(ROWS, COLS, CHANS)
    pre = hidden_pre.reshape(ROWS, COLS, CHANS)
    first = layer_input.reshape(ROWS, COLS, CHANS)
    near = lax.ppermute(own, mp, [(i, i ^ 1) for i in range(PLANES)])
    far = lax.ppermute(own, mp, [(i, i + (1 if i % 2 else -1)) for i in range(1, PLANES - 1)])
    core = lax.axis_index("c").reshape(1)
    kept = [pltpu.with_memory_space_constraint(a, pltpu.HBM) for a in (own, pre, first)]
    given = late(core, near, far, *early(*kept, weight_second))
    given = lax.all_to_all(given, mp, 0, 0, tiled=True)
    parts = weight_grad(given).astype(F16)
    parts = lax.all_to_all(parts, ("zl", "yh", "yl", "c"), 0, 0, tiled=True)
    mine = merge(parts.astype(F32)).astype(F16)
    sums = lax.all_gather(mine, "zh", axis=0, tiled=True).reshape(8, 4 * PIECE, 128)
    pieces = lax.all_to_all(finish(sums.astype(F32)), ("zl", "yl"), 0, 0, tiled=True)
    return tuple(unpack(pieces))


def solution(mesh):
    split = Mesh(mesh.devices.reshape(8, 4, 2, 4, 2, 2), ("zh", "zl", "yl", "x", "yh", "c"))
    dp, mp = ("zh", "zl", "yl"), ("x", "yh", "c")
    return jax.shard_map(
        local,
        mesh=split,
        in_specs=(P(dp, mp), P(dp, mp), P(dp, mp), P()),
        out_specs=(P(mp, None), P(mp, None)),
        check_vma=False,
    )
```
